32 devices in a mesh: parts: 2 (over y), tensor: 4 (over z), fsdp: 4 (over x, core).
Axes of the slice: x: 2, y: 2, z: 4, core: 2. Of those that a mesh axis runs over, the one named last changes fastest.
Arguments:
- tokens: bfloat16 [1024, 4096], P(('parts', 'fsdp'), 'tensor'), parts along dimension 0, may hold values from -6 to 6
- cotangent: bfloat16 [1024, 4096], P(('parts', 'fsdp'), 'tensor'), parts along dimension 0, may hold values from -6 to 6
- gate_values: bfloat16 [8, 160, 128, 128], P('fsdp', 'tensor'), may hold values from -0.1875 to 0.1875
- gate_rows: int32 [8, 160], P('fsdp', 'tensor'), may hold values from 0 to 31, as said below
- gate_scale: bfloat16 [8, 160], P('fsdp', 'tensor'), may hold values from 0.5 to 2
- up_values: bfloat16 [8, 160, 128, 128], P('fsdp', 'tensor'), may hold values from -0.1875 to 0.1875
- up_rows: int32 [8, 160], P('fsdp', 'tensor'), may hold values from 0 to 31, as said below
- up_scale: bfloat16 [8, 160], P('fsdp', 'tensor'), may hold values from 0.5 to 2
- down_values: bfloat16 [8, 160, 128, 128], P('fsdp', 'tensor'), may hold values from -0.078125 to 0.078125
- down_cols: int32 [8, 160], P('fsdp', 'tensor'), may hold values from 0 to 31, as said below
- down_scale: bfloat16 [8, 160], P('fsdp', 'tensor'), may hold values from 0.5 to 2
Outputs:
- layer_out: bfloat16 [1024, 4096], P(('parts', 'fsdp'), 'tensor'), parts along dimension 0
- grad_tokens: bfloat16 [1024, 4096], P(('parts', 'fsdp'), 'tensor'), parts along dimension 0
- grad_gate: bfloat16 [16, 160, 128, 128], P(('parts', 'fsdp'), 'tensor'), parts along dimension 0
- grad_up: bfloat16 [16, 160, 128, 128], P(('parts', 'fsdp'), 'tensor'), parts along dimension 0
- grad_down: bfloat16 [16, 160, 128, 128], P(('parts', 'fsdp'), 'tensor'), parts along dimension 0
The draws below stay inside these ranges and needn't reach their ends.
There are 2 independent parts, one for each index of `parts`. The reference program is written for one: setup_inputs(seed, part) draws one part's arguments, and reference() takes and returns one part's arrays. A program takes and returns all parts, laid end to end along the dimension named above; an argument that names none is the same for every part. Nothing has to cross between parts.
Inputs may be any that keep to these rules, and one draw needn't show every extreme that they name: `gate_rows`: the 8 entries of each column name distinct input blocks; some input blocks are named far more often than others. `up_rows`: the 8 entries of each column name distinct input blocks; some input blocks are named far more often than others. `down_cols`: the 8 entries of each column name distinct output blocks; some output blocks are named far more often than others.
All inputs are finite; a program needn't handle non-finite values.
Results may differ from the reference program's by a relative error of at most 0.023.
Values may be sent and summed in bfloat16 or wider, within the bound.
A program may use at most 192 MiB of HBM per device.

```python
import math
import jax
import jax.numpy as jnp
from jax import lax

D = 4096
FF = 20480
BLK = 128
K = 8
TOK_DEV = 128
TOKENS = 512
N_FSDP = 4


def pick_blocks(key):
    nblocks = D // BLK
    ncolumns = FF // BLK
    popular = jax.random.randint(jax.random.fold_in(key, 1), (nblocks,), 0, 1 << 20)
    noise = jax.random.randint(jax.random.fold_in(key, 2), (ncolumns, nblocks), 0, 1 << 20)
    column_ids = jnp.arange(ncolumns, dtype=jnp.int32)[:, None]
    block_ids = jnp.arange(nblocks, dtype=jnp.int32)[None, :]
    forced = (column_ids == 0) & (block_ids == 0) | (column_ids == 1) & (block_ids == nblocks - 1)
    scores = (noise + popular[None, :] + forced.astype(jnp.int32) * (1 << 22)) * nblocks + block_ids
    chosen = lax.top_k(scores, K)[1]
    return jnp.transpose(chosen).astype(jnp.int32)


def draw_gate_rows(key, part):
    return pick_blocks(jax.random.fold_in(key, 11))


def draw_up_rows(key, part):
    return pick_blocks(jax.random.fold_in(key, 12))


def draw_down_cols(key, part):
    return pick_blocks(jax.random.fold_in(key, 13))


def block_levels(own_key, shape, shards, smallest, largest):
    gain = 1.0
    for dim, shards_of in shards:
        steps = jax.random.uniform(jax.random.fold_in(jax.random.fold_in(own_key, 6), dim), (shards_of,), jnp.float32, smallest / len(shards), largest / len(shards))
        gain = gain * jnp.repeat(jnp.exp(steps), shape[dim] // shards_of).reshape((-1,) + (1,) * (len(shape) - 1 - dim))
    return gain


def normal_values(rng, dims, scale, limit, shards=(), kind=jnp.bfloat16):
    values = jax.random.normal(rng, dims, jnp.float32) * scale
    if len(shards) > 0:
        values = block_levels(rng, dims, shards, -0.22, 0.18) * values
    return jnp.clip(values, min=-limit, max=limit).astype(kind)


def setup_inputs(seed: int = 0, part: int = 0) -> dict:
    seeds = jax.random.split(jax.random.key(seed), 12)
    part_splits = jax.random.split(jax.random.fold_in(seeds[11], part), 12)
    tokens = normal_values(part_splits[0], (TOKENS, D), 1.0, 6.0, ((0, 4), (1, 4)))
    cotangent = normal_values(part_splits[1], (TOKENS, D), 0.5, 6.0, ((0, 4), (1, 4)))
    gate_values = normal_values(seeds[2], (K, FF // BLK, BLK, BLK), (K * BLK) ** -0.5, 0.1875, ((0, 4), (1, 4)))
    gate_rows = draw_gate_rows(jax.random.fold_in(seeds[11], 71), part)
    gate_scale = jnp.clip(jnp.exp(math.log(2.0) - 1.3862944 * jax.random.uniform(seeds[4], (K, FF // BLK), jnp.float32) ** block_levels(seeds[4], (K, FF // BLK), ((0, 4), (1, 4)), -0.2, 0.2)), 0.5, 2.0).astype(jnp.bfloat16)
    up_values = normal_values(seeds[5], (K, FF // BLK, BLK, BLK), (K * BLK) ** -0.5, 0.1875, ((0, 4), (1, 4)))
    up_rows = draw_up_rows(jax.random.fold_in(seeds[11], 71), part)
    up_scale = jnp.clip(jnp.exp(math.log(2.0) - 1.3862944 * jax.random.uniform(seeds[7], (K, FF // BLK), jnp.float32) ** block_levels(seeds[7], (K, FF // BLK), ((0, 4), (1, 4)), -0.2, 0.2)), 0.5, 2.0).astype(jnp.bfloat16)
    down_values = normal_values(seeds[8], (K, FF // BLK, BLK, BLK), (FF * K // (D // BLK)) ** -0.5, 0.078125, ((0, 4), (1, 4)))
    down_cols = draw_down_cols(jax.random.fold_in(seeds[11], 71), part)
    down_scale = jnp.clip(jnp.exp(math.log(2.0) - 1.3862944 * jax.random.uniform(seeds[10], (K, FF // BLK), jnp.float32) ** block_levels(seeds[10], (K, FF // BLK), ((0, 4), (1, 4)), -0.2, 0.2)), 0.5, 2.0).astype(jnp.bfloat16)
    return dict(tokens=tokens, cotangent=cotangent, gate_values=gate_values, gate_rows=gate_rows, gate_scale=gate_scale, up_values=up_values, up_rows=up_rows, up_scale=up_scale, down_values=down_values, down_cols=down_cols, down_scale=down_scale)


def weighted(selected, blocks, factors):
    products = jnp.einsum('tka,kab->tkb', selected, blocks.astype(jnp.float32))
    return jnp.sum(products * factors.astype(jnp.float32)[None, :, None], axis=1)


def rounded(values):
    return lax.optimization_barrier(values.astype(jnp.bfloat16)).astype(jnp.float32)


def group_sum(left, right, form, factors):
    left_groups = left.reshape((N_FSDP, TOK_DEV) + left.shape[1:])
    right_groups = right.reshape((N_FSDP, TOK_DEV) + right.shape[1:])
    terms = jnp.einsum(form, left_groups, right_groups) * factors.astype(jnp.float32)[None, :, None, None]
    return jnp.sum(rounded(terms), axis=0)


def reference(tokens, cotangent, gate_values, gate_rows, gate_scale, up_values, up_rows, up_scale, down_values, down_cols, down_scale):
    nblocks = D // BLK
    token_total = TOKENS
    x_blocks = tokens.reshape(token_total, nblocks, BLK).astype(jnp.float32)
    grad_blocks = cotangent.reshape(token_total, nblocks, BLK).astype(jnp.float32)
    columns = tuple(jnp.swapaxes(item, 0, 1) for item in (gate_values, gate_rows, gate_scale, up_values, up_rows, up_scale, down_values, down_cols, down_scale))

    def forward(out_sum, column):
        gate_blocks, gate_where, gate_factor, up_blocks, up_where, up_factor, down_blocks, down_where, down_factor = column
        gate_pre = weighted(x_blocks[:, gate_where], gate_blocks, gate_factor)
        up_pre = weighted(x_blocks[:, up_where], up_blocks, up_factor)
        hidden = rounded(gate_pre * jax.nn.sigmoid(gate_pre) * up_pre)
        pieces = jnp.einsum('tb,kbc->tkc', hidden, down_blocks.astype(jnp.float32)) * down_factor.astype(jnp.float32)[None, :, None]
        out_sum = out_sum.at[:, down_where].add(pieces)
        return out_sum, (gate_pre, up_pre, hidden)

    empty_sum = jnp.zeros((token_total, nblocks, BLK), jnp.float32)
    out_sum, saved = lax.scan(forward, empty_sum, columns)
    layer_out = out_sum.reshape(token_total, D).astype(jnp.bfloat16)

    def backward(in_sum, inputs):
        column, kept = inputs
        gate_blocks, gate_where, gate_factor, up_blocks, up_where, up_factor, down_blocks, down_where, down_factor = column
        gate_pre, up_pre, hidden = kept
        down_sel = grad_blocks[:, down_where]
        grad_hidden = jnp.sum(jnp.einsum('tkc,kbc->tkb', down_sel, down_blocks.astype(jnp.float32)) * down_factor.astype(jnp.float32)[None, :, None], axis=1)
        sigmoid_gate = jax.nn.sigmoid(gate_pre)
        grad_gate_act = rounded(grad_hidden * up_pre * sigmoid_gate * (1.0 + gate_pre * (1.0 - sigmoid_gate)))
        grad_up_act = rounded(grad_hidden * gate_pre * sigmoid_gate)
        gate_sel = x_blocks[:, gate_where]
        up_sel = x_blocks[:, up_where]
        down_part = group_sum(hidden, down_sel, 'qtb,qtkc->qkbc', down_factor)
        gate_part = group_sum(gate_sel, grad_gate_act, 'qtka,qtb->qkab', gate_factor)
        up_part = group_sum(up_sel, grad_up_act, 'qtka,qtb->qkab', up_factor)
        back_gate = jnp.einsum('tb,kab->tka', grad_gate_act, gate_blocks.astype(jnp.float32)) * gate_factor.astype(jnp.float32)[None, :, None]
        back_up = jnp.einsum('tb,kab->tka', grad_up_act, up_blocks.astype(jnp.float32)) * up_factor.astype(jnp.float32)[None, :, None]
        in_sum = in_sum.at[:, gate_where].add(back_gate)
        in_sum = in_sum.at[:, up_where].add(back_up)
        return in_sum, (gate_part, up_part, down_part)

    in_sum, grads = lax.scan(backward, empty_sum, (columns, saved))
    grad_tokens = in_sum.reshape(token_total, D).astype(jnp.bfloat16)
    grad_gate = jnp.swapaxes(grads[0], 0, 1).astype(jnp.bfloat16)
    grad_up = jnp.swapaxes(grads[1], 0, 1).astype(jnp.bfloat16)
    grad_down = jnp.swapaxes(grads[2], 0, 1).astype(jnp.bfloat16)
    return (layer_out, grad_tokens, grad_gate, grad_up, grad_down)
```

```python
import functools

import jax
import jax.numpy as jnp
from jax import lax
from jax.experimental import pallas as pl
from jax.experimental.pallas import tpu as pltpu
from jax.sharding import PartitionSpec as P


def scaled_sum(products, factors):
    return jnp.sum(products * factors.astype(jnp.float32)[None, :, :, None], axis=1)


def slot_term(selected, grads, factors):
    return (
        jnp.einsum("tkra,trb->krab", selected, grads, preferred_element_type=jnp.float32)
        * factors[:, :, None, None]
    )


def gathered_plan(
    tokens,
    cotangent,
    gate_values,
    gate_rows,
    gate_scale,
    up_values,
    up_rows,
    up_scale,
    down_values,
    down_cols,
    down_scale,
):
    block_size = gate_values.shape[-1]
    token_count = tokens.shape[0]
    tensor_count = lax.axis_size("tensor")
    nblocks = tokens.shape[1] * tensor_count // block_size
    local_blocks = nblocks // tensor_count
    gathered = lax.all_gather(tokens, "tensor", axis=1, tiled=True)
    x_blocks = gathered.reshape(token_count, nblocks, block_size)
    gate_where, up_where, down_where = (
        lax.all_gather(gate_rows, "fsdp", axis=0, tiled=True),
        lax.all_gather(up_rows, "fsdp", axis=0, tiled=True),
        lax.all_gather(down_cols, "fsdp", axis=0, tiled=True),
    )
    gate_blocks, gate_factor, up_blocks, up_factor, down_blocks, down_factor = (
        lax.all_gather(gate_values, "fsdp", axis=0, tiled=True),
        lax.all_gather(gate_scale, "fsdp", axis=0, tiled=True),
        lax.all_gather(up_values, "fsdp", axis=0, tiled=True),
        lax.all_gather(up_scale, "fsdp", axis=0, tiled=True),
        lax.all_gather(down_values, "fsdp", axis=0, tiled=True),
        lax.all_gather(down_scale, "fsdp", axis=0, tiled=True),
    )
    gate_sel = x_blocks[:, gate_where]
    up_sel = x_blocks[:, up_where]
    gate_pre = scaled_sum(
        jnp.einsum("tkra,krab->tkrb", gate_sel, gate_blocks, preferred_element_type=jnp.float32),
        gate_factor,
    )
    up_pre = scaled_sum(
        jnp.einsum("tkra,krab->tkrb", up_sel, up_blocks, preferred_element_type=jnp.float32),
        up_factor,
    )
    sigmoid_gate = jax.nn.sigmoid(gate_pre)
    activated = gate_pre * sigmoid_gate
    hidden = (activated * up_pre).astype(jnp.bfloat16)
    down_float = down_factor.astype(jnp.float32)
    down_scaled = (
        jnp.einsum("trb,krbc->krtc", hidden, down_blocks, preferred_element_type=jnp.float32)
        * down_float[:, :, None, None]
    )
    out_full = (
        jnp.zeros((nblocks, token_count, block_size), jnp.float32).at[down_where].add(down_scaled)
    )
    out_part = lax.psum_scatter(
        out_full.astype(jnp.bfloat16), "tensor", scatter_dimension=0, tiled=True
    ).astype(jnp.float32)
    layer_out = (
        jnp.transpose(out_part, (1, 0, 2))
        .reshape(token_count, local_blocks * block_size)
        .astype(jnp.bfloat16)
    )
    grad_full = lax.all_gather(cotangent, "tensor", axis=1, tiled=True).reshape(
        token_count, nblocks, block_size
    )
    down_sel = grad_full[:, down_where]
    gate_float = gate_factor.astype(jnp.float32)
    up_float = up_factor.astype(jnp.float32)
    grad_hidden = scaled_sum(
        jnp.einsum("tkrc,krbc->tkrb", down_sel, down_blocks, preferred_element_type=jnp.float32),
        down_factor,
    )
    grad_down = lax.psum_scatter(
        (
            jnp.einsum("trb,tkrc->krbc", hidden, down_sel, preferred_element_type=jnp.float32)
            * down_float[:, :, None, None]
        ).astype(jnp.bfloat16),
        "fsdp",
        scatter_dimension=0,
        tiled=True,
    )
    grad_gate_act = (
        grad_hidden * up_pre * sigmoid_gate * (1.0 + gate_pre * (1.0 - sigmoid_gate))
    ).astype(jnp.bfloat16)
    grad_up_act = (grad_hidden * activated).astype(jnp.bfloat16)
    grad_gate = lax.psum_scatter(
        slot_term(gate_sel, grad_gate_act, gate_float).astype(jnp.bfloat16),
        "fsdp",
        scatter_dimension=0,
        tiled=True,
    )
    grad_up = lax.psum_scatter(
        slot_term(up_sel, grad_up_act, up_float).astype(jnp.bfloat16),
        "fsdp",
        scatter_dimension=0,
        tiled=True,
    )
    back_gate = (
        jnp.einsum("trb,krab->krta", grad_gate_act, gate_blocks, preferred_element_type=jnp.float32)
        * gate_float[:, :, None, None]
    )
    back_up = (
        jnp.einsum("trb,krab->krta", grad_up_act, up_blocks, preferred_element_type=jnp.float32)
        * up_float[:, :, None, None]
    )
    in_full = (
        jnp.zeros((nblocks, token_count, block_size), jnp.float32)
        .at[gate_where]
        .add(back_gate)
        .at[up_where]
        .add(back_up)
    )
    in_part = lax.psum_scatter(
        in_full.astype(jnp.bfloat16), "tensor", scatter_dimension=0, tiled=True
    ).astype(jnp.float32)
    grad_tokens = (
        jnp.transpose(in_part, (1, 0, 2))
        .reshape(token_count, local_blocks * block_size)
        .astype(jnp.bfloat16)
    )
    return (layer_out, grad_tokens, grad_gate, grad_up, grad_down)


def column_kernel(
    shape,
    rows_ref,
    scale_ref,
    near_ref,
    far_ref,
    *refs,
):
    slots, per_dev, nblk, blk, tok = shape
    nsrc = slots // per_dev
    weight_refs = [refs[i * nsrc : (i + 1) * nsrc] for i in range(3)]
    grad_refs = [refs[(3 + i) * nsrc : (4 + i) * nsrc] for i in range(3)]
    own_ref, other_ref = refs[6 * nsrc : 6 * nsrc + 2]
    (out_acc, in_acc, gate_sel, up_sel, down_sel, gate_w, up_w, down_w) = refs[6 * nsrc + 2 :]
    r = pl.program_id(0)
    per_shard = near_ref.shape[3]

    @pl.when(r == 0)
    def _():
        out_acc[...] = jnp.zeros_like(out_acc)
        in_acc[...] = jnp.zeros_like(in_acc)

    def load(which, slot, array, sel):
        place = rows_ref[array, slot, r]
        shard, block = place // per_shard, place % per_shard
        lanes = slice(slot * blk, (slot + 1) * blk)
        for c, ref in enumerate((near_ref, far_ref)):
            for x in range(2):
                q = c * 2 + x
                sel[q * tok : (q + 1) * tok, lanes] = ref[shard, x, which, block]

    def scaled(array, slot):
        value = weight_refs[array][slot // per_dev][slot % per_dev, 0]
        return (value.astype(jnp.float32) * scale_ref[array, slot, r]).astype(jnp.bfloat16)

    for slot in range(slots):
        span = slice(slot * blk, (slot + 1) * blk)
        load(0, slot, 0, gate_sel)
        load(0, slot, 1, up_sel)
        load(1, slot, 2, down_sel)
        gate_w[span, :] = scaled(0, slot)
        up_w[span, :] = scaled(1, slot)
        down_w[:, span] = scaled(2, slot)

    nn = (((1,), (0,)), ((), ()))
    nt = (((1,), (1,)), ((), ()))
    dot = functools.partial(lax.dot_general, preferred_element_type=jnp.float32)
    gate_pre = dot(gate_sel[...], gate_w[...], nn)
    up_pre = dot(up_sel[...], up_w[...], nn)
    grad_hidden = dot(down_sel[...], down_w[...], nt)
    sig = jax.nn.sigmoid(gate_pre)
    act = gate_pre * sig
    hidden = (act * up_pre).astype(jnp.bfloat16)
    gate_act = (grad_hidden * up_pre * sig * (1.0 + gate_pre * (1.0 - sig))).astype(jnp.bfloat16)
    up_act = (grad_hidden * act).astype(jnp.bfloat16)

    for slot in range(slots):
        span = slice(slot * blk, (slot + 1) * blk)
        src, sub = slot // per_dev, slot % per_dev
        g = dot(gate_sel[:, span].T, gate_act, nn) * scale_ref[0, slot, r]
        grad_refs[0][src][sub, 0] = g.astype(jnp.bfloat16)
        g = dot(up_sel[:, span].T, up_act, nn) * scale_ref[1, slot, r]
        grad_refs[1][src][sub, 0] = g.astype(jnp.bfloat16)
    hidden_t = hidden.T
    down = dot(hidden_t, down_sel[...], nn)
    for slot in range(slots):
        src, sub = slot // per_dev, slot % per_dev
        g = down[:, slot * blk : (slot + 1) * blk] * scale_ref[2, slot, r]
        grad_refs[2][src][sub, 0] = g.astype(jnp.bfloat16)

    for array, acc, left, w in ((0, in_acc, gate_act, gate_w), (1, in_acc, up_act, up_w), (2, out_acc, hidden, down_w)):
        product = dot(left, w[...], nn if array == 2 else nt)
        for slot in range(slots):
            place = rows_ref[array, slot, r]
            acc[place] += product[:, slot * blk : (slot + 1) * blk]

    @pl.when(r == pl.num_programs(0) - 1)
    def _():
        for which, acc in enumerate((out_acc, in_acc)):
            for c, ref in enumerate((own_ref, other_ref)):
                for x in range(2):
                    q = c * 2 + x

                    @pl.loop(0, nblk)
                    def _(d):
                        ref[d // per_shard, which, x, d % per_shard] = acc[d, q * tok : (q + 1) * tok, :].astype(jnp.bfloat16)


def columns(table_rows, table_scale, near, far, weights, own):
    nsrc = len(weights[0])
    per_dev, count, blk, _ = weights[0][1].shape
    shards, _, _, per_shard, tok, _ = near.shape
    nblk = shards * per_shard
    slots = per_dev * nsrc
    total = 4 * tok
    whole = lambda a: pl.BlockSpec(a, lambda r, *_: (0,) * len(a), pipeline_mode=pl.Buffered(1))
    block = pl.BlockSpec((per_dev, 1, blk, blk), lambda r, *_: (0, r, 0, 0))
    piece = jax.ShapeDtypeStruct((per_dev, count, blk, blk), jnp.bfloat16)
    out_block = (shards, 2, 2, per_shard, tok, blk)
    bf = jnp.bfloat16
    flops = 2 * 9 * slots * count * total * blk * blk
    outs = pl.pallas_call(
        functools.partial(column_kernel, (slots, per_dev, nblk, blk, tok)),
        grid_spec=pltpu.PrefetchScalarGridSpec(
            num_scalar_prefetch=2,
            grid=(count,),
            in_specs=[whole(near.shape), whole(far.shape)] + [block] * (3 * nsrc),
            out_specs=[block] * (3 * nsrc) + [whole(out_block)] * 2,
            scratch_shapes=[
                pltpu.VMEM((nblk, total, blk), jnp.float32),
                pltpu.VMEM((nblk, total, blk), jnp.float32),
                pltpu.VMEM((total, slots * blk), bf),
                pltpu.VMEM((total, slots * blk), bf),
                pltpu.VMEM((total, slots * blk), bf),
                pltpu.VMEM((slots * blk, blk), bf),
                pltpu.VMEM((slots * blk, blk), bf),
                pltpu.VMEM((blk, slots * blk), bf),
            ],
        ),
        out_shape=[piece] * (3 * nsrc) + [jax.ShapeDtypeStruct(out_block, bf)] * 2,
        compiler_params=pltpu.CompilerParams(vmem_limit_bytes=60 * 1024 * 1024),
        cost_estimate=pl.CostEstimate(flops=2 * flops, bytes_accessed=40 << 20, transcendentals=0),
    )(table_rows, table_scale, near, far, *weights[0], *weights[1], *weights[2])
    grads = [outs[i * nsrc : (i + 1) * nsrc] for i in range(3)]
    return grads, outs[3 * nsrc], outs[3 * nsrc + 1]


def swap(value, flip):
    return lax.ppermute(value, "fsdp", [(i, i ^ flip) for i in range(4)])


def exchanged_plan(
    tokens,
    cotangent,
    gate_values,
    gate_rows,
    gate_scale,
    up_values,
    up_rows,
    up_scale,
    down_values,
    down_cols,
    down_scale,
):
    tok, width = tokens.shape
    per_dev, local_cols, blk, _ = gate_values.shape
    count = local_cols // 4
    mine = lax.axis_index("fsdp")
    f32, bf = jnp.float32, jnp.bfloat16

    both = jnp.stack([tokens, cotangent]).reshape(2, tok, width // blk, blk).transpose(0, 2, 1, 3)
    both = jnp.stack([both, swap(both, 2)])
    near = lax.all_gather(both, "tensor", axis=0)
    far = swap(near, 1)

    def piece(values, flip):
        return lax.dynamic_slice_in_dim(values, (mine ^ flip) * count, count, axis=-3)

    small = jnp.stack(
        [a.astype(f32) for a in (gate_rows, up_rows, down_cols, gate_scale, up_scale, down_scale)]
    )

    def small_piece(flip):
        return lax.dynamic_slice_in_dim(small, (mine ^ flip) * count, count, axis=2)

    tables = jnp.concatenate(
        [small_piece(0)] + [swap(small_piece(m), m) for m in (1, 2, 3)], axis=1
    )
    table_rows = tables[:3].astype(jnp.int32)
    table_scale = tables[3:]
    weights = [
        [piece(v, 0)] + [swap(piece(v, m), m) for m in (1, 2, 3)]
        for v in (gate_values, up_values, down_values)
    ]
    grads, own, other = columns(table_rows, table_scale, near, far, weights, mine)

    def home(pieces):
        result = jnp.zeros((per_dev, local_cols, blk, blk), bf)
        for m, part in enumerate(pieces):
            part = part if m == 0 else swap(part, m)
            result = lax.dynamic_update_slice_in_dim(result, part, (mine ^ m) * count, axis=1)
        return result

    grad_gate, grad_up, grad_down = [home(p) for p in grads]
    chip = (own.astype(f32) + swap(other, 1).astype(f32)).astype(bf)
    shard = lax.psum_scatter(chip, "tensor", scatter_dimension=0, tiled=False)
    done = (shard[:, 0].astype(f32) + swap(shard[:, 1], 2).astype(f32)).astype(bf)
    done = done.transpose(0, 2, 1, 3).reshape(2, tok, width)
    return (done[0], done[1], grad_gate, grad_up, grad_down)


def choose_plan(mesh, *args):
    shards, columns_here = mesh.shape["fsdp"], args[2].shape[1]
    plan = exchanged_plan if shards == 4 and columns_here % shards == 0 else gathered_plan
    return plan(*args)


def solution(mesh):
    plan = functools.partial(choose_plan, mesh)
    in_specs = (
        P(("parts", "fsdp"), "tensor"),
        P(("parts", "fsdp"), "tensor"),
        P("fsdp", "tensor", None, None),
        P("fsdp", "tensor"),
        P("fsdp", "tensor"),
        P("fsdp", "tensor", None, None),
        P("fsdp", "tensor"),
        P("fsdp", "tensor"),
        P("fsdp", "tensor", None, None),
        P("fsdp", "tensor"),
        P("fsdp", "tensor"),
    )
    out_specs = (
        P(("parts", "fsdp"), "tensor"),
        P(("parts", "fsdp"), "tensor"),
        P(("parts", "fsdp"), "tensor", None, None),
        P(("parts", "fsdp"), "tensor", None, None),
        P(("parts", "fsdp"), "tensor", None, None),
    )
    return jax.shard_map(plan, mesh=mesh, in_specs=in_specs, out_specs=out_specs, check_vma=False)
```

```python
import functools

import jax
import jax.numpy as jnp
from jax import lax
from jax.experimental import pallas as pl
from jax.experimental.pallas import tpu as pltpu
from jax.sharding import PartitionSpec as P


def scaled_sum(products, factors):
    return jnp.sum(products * factors.astype(jnp.float32)[None, :, :, None], axis=1)


def slot_term(selected, grads, factors):
    return (
        jnp.einsum("tkra,trb->krab", selected, grads, preferred_element_type=jnp.float32)
        * factors[:, :, None, None]
    )


def gathered_plan(
    tokens,
    cotangent,
    gate_values,
    gate_rows,
    gate_scale,
    up_values,
    up_rows,
    up_scale,
    down_values,
    down_cols,
    down_scale,
):
    block_size = gate_values.shape[-1]
    token_count = tokens.shape[0]
    tensor_count = lax.axis_size("tensor")
    nblocks = tokens.shape[1] * tensor_count // block_size
    local_blocks = nblocks // tensor_count
    gathered = lax.all_gather(tokens, "tensor", axis=1, tiled=True)
    x_blocks = gathered.reshape(token_count, nblocks, block_size)
    gate_where, up_where, down_where = (
        lax.all_gather(gate_rows, "fsdp", axis=0, tiled=True),
        lax.all_gather(up_rows, "fsdp", axis=0, tiled=True),
        lax.all_gather(down_cols, "fsdp", axis=0, tiled=True),
    )
    gate_blocks, gate_factor, up_blocks, up_factor, down_blocks, down_factor = (
        lax.all_gather(gate_values, "fsdp", axis=0, tiled=True),
        lax.all_gather(gate_scale, "fsdp", axis=0, tiled=True),
        lax.all_gather(up_values, "fsdp", axis=0, tiled=True),
        lax.all_gather(up_scale, "fsdp", axis=0, tiled=True),
        lax.all_gather(down_values, "fsdp", axis=0, tiled=True),
        lax.all_gather(down_scale, "fsdp", axis=0, tiled=True),
    )
    gate_sel = x_blocks[:, gate_where]
    up_sel = x_blocks[:, up_where]
    gate_pre = scaled_sum(
        jnp.einsum("tkra,krab->tkrb", gate_sel, gate_blocks, preferred_element_type=jnp.float32),
        gate_factor,
    )
    up_pre = scaled_sum(
        jnp.einsum("tkra,krab->tkrb", up_sel, up_blocks, preferred_element_type=jnp.float32),
        up_factor,
    )
    sigmoid_gate = jax.nn.sigmoid(gate_pre)
    activated = gate_pre * sigmoid_gate
    hidden = (activated * up_pre).astype(jnp.bfloat16)
    down_float = down_factor.astype(jnp.float32)
    down_scaled = (
        jnp.einsum("trb,krbc->krtc", hidden, down_blocks, preferred_element_type=jnp.float32)
        * down_float[:, :, None, None]
    )
    out_full = (
        jnp.zeros((nblocks, token_count, block_size), jnp.float32).at[down_where].add(down_scaled)
    )
    out_part = lax.psum_scatter(
        out_full.astype(jnp.bfloat16), "tensor", scatter_dimension=0, tiled=True
    ).astype(jnp.float32)
    layer_out = (
        jnp.transpose(out_part, (1, 0, 2))
        .reshape(token_count, local_blocks * block_size)
        .astype(jnp.bfloat16)
    )
    grad_full = lax.all_gather(cotangent, "tensor", axis=1, tiled=True).reshape(
        token_count, nblocks, block_size
    )
    down_sel = grad_full[:, down_where]
    gate_float = gate_factor.astype(jnp.float32)
    up_float = up_factor.astype(jnp.float32)
    grad_hidden = scaled_sum(
        jnp.einsum("tkrc,krbc->tkrb", down_sel, down_blocks, preferred_element_type=jnp.float32),
        down_factor,
    )
    grad_down = lax.psum_scatter(
        (
            jnp.einsum("trb,tkrc->krbc", hidden, down_sel, preferred_element_type=jnp.float32)
            * down_float[:, :, None, None]
        ).astype(jnp.bfloat16),
        "fsdp",
        scatter_dimension=0,
        tiled=True,
    )
    grad_gate_act = (
        grad_hidden * up_pre * sigmoid_gate * (1.0 + gate_pre * (1.0 - sigmoid_gate))
    ).astype(jnp.bfloat16)
    grad_up_act = (grad_hidden * activated).astype(jnp.bfloat16)
    grad_gate = lax.psum_scatter(
        slot_term(gate_sel, grad_gate_act, gate_float).astype(jnp.bfloat16),
        "fsdp",
        scatter_dimension=0,
        tiled=True,
    )
    grad_up = lax.psum_scatter(
        slot_term(up_sel, grad_up_act, up_float).astype(jnp.bfloat16),
        "fsdp",
        scatter_dimension=0,
        tiled=True,
    )
    back_gate = (
        jnp.einsum("trb,krab->krta", grad_gate_act, gate_blocks, preferred_element_type=jnp.float32)
        * gate_float[:, :, None, None]
    )
    back_up = (
        jnp.einsum("trb,krab->krta", grad_up_act, up_blocks, preferred_element_type=jnp.float32)
        * up_float[:, :, None, None]
    )
    in_full = (
        jnp.zeros((nblocks, token_count, block_size), jnp.float32)
        .at[gate_where]
        .add(back_gate)
        .at[up_where]
        .add(back_up)
    )
    in_part = lax.psum_scatter(
        in_full.astype(jnp.bfloat16), "tensor", scatter_dimension=0, tiled=True
    ).astype(jnp.float32)
    grad_tokens = (
        jnp.transpose(in_part, (1, 0, 2))
        .reshape(token_count, local_blocks * block_size)
        .astype(jnp.bfloat16)
    )
    return (layer_out, grad_tokens, grad_gate, grad_up, grad_down)


SPLIT = 5


def gather_kernel(shards, small, both, wg, wu, wd, tok_all, rg, ru, rd, table, *sems):
    (z_send, z_recv, c_send, c_recv, x_send, x_recv, w_send, w_recv, y_send, y_recv, n_send, n_recv, s_send, s_recv, here) = sems
    part, t, f = lax.axis_index("parts"), lax.axis_index("tensor"), lax.axis_index("fsdp")
    flip = [f, (f // 2) * 2 + 1 - f % 2, (f + 2) % 4, ((f + 2) % 4 // 2) * 2 + 1 - f % 2]
    count = rg.shape[2]
    last = shards - 1
    weights = ((wg, rg), (wu, ru), (wd, rd))

    def to(where, src, dst, send, recv):
        return pltpu.make_async_remote_copy(
            src_ref=src, dst_ref=dst, send_sem=send, recv_sem=recv,
            device_id=where, device_id_type=pl.DeviceIdType.MESH,
        )

    def across(m):
        return (part, t, flip[m])

    over = (1 - part, t, f)
    ups = ((part, t + 1, f), (part, t - 1, f))
    more = (t < last, t > 0)

    barrier = pltpu.get_barrier_semaphore()
    for m in (1, 2, 3):
        pl.semaphore_signal(barrier, inc=1, device_id=across(m), device_id_type=pl.DeviceIdType.MESH)
    pl.semaphore_signal(barrier, inc=1, device_id=over, device_id_type=pl.DeviceIdType.MESH)
    for way in range(2):
        @pl.when(more[way])
        def _():
            pl.semaphore_signal(barrier, inc=1, device_id=ups[way], device_id_type=pl.DeviceIdType.MESH)
    ends = jnp.logical_or(t == 0, t == last)

    @pl.when(ends)
    def _():
        pl.semaphore_wait(barrier, 5)

    @pl.when(jnp.logical_not(ends))
    def _():
        pl.semaphore_wait(barrier, 6)

    def z_copy(way, src, x, own=False):
        source = both if own else tok_all.at[0, src, x]
        return to(ups[way], source, tok_all.at[0, src, x], z_send.at[way, src, x], z_recv.at[way, src, x])

    def c_copy(src, x, own=False):
        source = both if own else tok_all.at[0, src, x]
        return to(across(1), source, tok_all.at[1, src, x], c_send.at[src, x], c_recv.at[src, x])

    x_copy = to(across(2), both, tok_all.at[0, t, 1], x_send, x_recv)
    keep = pltpu.make_async_copy(both, tok_all.at[0, t, 0], here)
    x_copy.start()
    for way in range(2):
        @pl.when(more[way])
        def _():
            z_copy(way, t, 0, True).start()
    tables = [
        to(across(m), small.at[flip[m]], table.at[m - 1], s_send.at[m - 1], s_recv.at[m - 1])
        for m in (1, 2, 3)
    ]
    for c in tables:
        c.start()
    c_copy(t, 0, True).start()
    w_copies, y_copies, y_waits, n_copies = [], [], [], []
    for w, r in weights:
        for m in (2, 3):
            j = len(w_copies)
            w_copies.append(to(across(m), w.at[part, pl.ds(flip[m] * count, count)], r.at[m - 1, part], w_send.at[j], w_recv.at[j]))
            y_copies.append(to(over, r.at[m - 1, part], r.at[m - 1, part], y_send.at[j], y_recv.at[j]))
            y_waits.append(to(over, r.at[m - 1, part], r.at[m - 1, 1 - part], y_send.at[j], y_recv.at[j]))
        for k in range(2):
            j = len(n_copies)
            n_copies.append(to(across(1), w.at[k, pl.ds(flip[1] * count, count)], r.at[0, k], n_send.at[j], n_recv.at[j]))
    for c in w_copies:
        c.start()
    for c in n_copies:
        c.start()
    keep.start()

    x_copy.wait_recv()
    for way in range(2):
        @pl.when(more[way])
        def _():
            z_copy(way, t, 1).start()
    c_copy(t, 1).start()

    def arrive(step, x):
        for way in range(2):
            src = t - step if way == 0 else t + step

            @pl.when(src >= 0 if way == 0 else src <= last)
            def _():
                z_copy(way, src, x).wait_recv()

                @pl.when(more[way])
                def _():
                    z_copy(way, src, x).start()

                c_copy(src, x).start()

    def relay(j):
        w_copies[j].wait_recv()
        y_copies[j].start()

    order = [(s, x) for s in range(1, shards) for x in range(2)]
    done = 0
    for i, (s, x) in enumerate(order):
        arrive(s, x)
        while done < len(w_copies) and done < 2 * i + 1:
            relay(done)
            done += 1
    while done < len(w_copies):
        relay(done)
        done += 1

    for way in range(2):
        for s in range(shards):
            src = t - s if way == 0 else t + s

            @pl.when(jnp.logical_and(src >= 0 if way == 0 else src <= last, more[way]))
            def _():
                for x in range(2):
                    z_copy(way, src, x, s == 0 and x == 0).wait_send()
    for src in range(shards):
        for x in range(2):
            c_copy(src, x).wait_send()
            c_copy(src, x).wait_recv()
    for c in tables + n_copies:
        c.wait_send()
        c.wait_recv()
    x_copy.wait_send()
    for c in w_copies + y_copies:
        c.wait_send()
    for c in y_waits:
        c.wait_recv()
    keep.wait()


def gather(small, both, weights, shards):
    per_dev, local_cols, blk, _ = weights[0].shape
    count = local_cols // 4
    bf = jnp.bfloat16
    dma = lambda *a: pltpu.SemaphoreType.DMA(a)
    received = jax.ShapeDtypeStruct((3, per_dev, count, blk, blk), bf)
    anywhere = pl.BlockSpec(memory_space=pl.ANY)
    z = (2, shards, 2)
    c = (shards, 2)
    one = pltpu.SemaphoreType.DMA
    return pl.pallas_call(
        functools.partial(gather_kernel, shards),
        out_shape=[
            jax.ShapeDtypeStruct((2, shards, 2) + both.shape, bf),
            received, received, received,
            jax.ShapeDtypeStruct((3,) + small.shape[1:], jnp.float32),
        ],
        in_specs=[anywhere] * 5,
        out_specs=[anywhere] * 5,
        scratch_shapes=[dma(*z), dma(*z), dma(*c), dma(*c), one, one, dma(6), dma(6), dma(6), dma(6), dma(6), dma(6), dma(3), dma(3), one],
        compiler_params=pltpu.CompilerParams(collective_id=0, has_side_effects=True),
    )(small, both, *weights)


def column_kernel(
    shape,
    rows_ref,
    scale_ref,
    mine_ref,
    tok_ref,
    *refs,
):
    slots, per_dev, nblk, blk, tok, base, nprev = shape
    nsrc = slots // per_dev
    prev_refs, refs = refs[:nprev], refs[nprev:]
    own_w, recv_w = refs[:3], refs[3:6]
    grad_refs = [refs[6 + i * nsrc : 6 + (1 + i) * nsrc] for i in range(3)]
    own_ref, other_ref = refs[3 * nsrc + 6 : 3 * nsrc + 8]
    (out_acc, in_acc, gate_sel, up_sel, down_sel, gate_w, up_w, down_w) = refs[3 * nsrc + 8 :]
    step = pl.program_id(0)
    r = step + base
    per_shard = tok_ref.shape[4]

    @pl.when(step == 0)
    def _():
        if not nprev:
            out_acc[...] = jnp.zeros_like(out_acc)
            in_acc[...] = jnp.zeros_like(in_acc)
            return
        for which, acc in enumerate((out_acc, in_acc)):
            for c, ref in enumerate(prev_refs):
                for x in range(2):
                    q = c * 2 + x

                    @pl.loop(0, nblk)
                    def _(d):
                        acc[d, q * tok : (q + 1) * tok, :] = ref[d // per_shard, which, x, d % per_shard].astype(jnp.float32)

    def load(which, slot, array, sel):
        place = rows_ref[array, slot, r]
        shard, block = place // per_shard, place % per_shard
        lanes = slice(slot * blk, (slot + 1) * blk)
        for c in range(2):
            for x in range(2):
                q = c * 2 + x
                sel[q * tok : (q + 1) * tok, lanes] = tok_ref[c, shard, x, which, block]

    def scaled(array, slot):
        src, sub = slot // per_dev, slot % per_dev
        value = recv_w[array][src - 1, sub, 0] if src else own_w[array][sub, 0]
        return (value.astype(jnp.float32) * scale_ref[array, slot, r]).astype(jnp.bfloat16)

    for slot in range(slots):
        span = slice(slot * blk, (slot + 1) * blk)
        load(0, slot, 0, gate_sel)
        load(0, slot, 1, up_sel)
        load(1, slot, 2, down_sel)
        gate_w[span, :] = scaled(0, slot)
        up_w[span, :] = scaled(1, slot)
        down_w[:, span] = scaled(2, slot)

    nn = (((1,), (0,)), ((), ()))
    nt = (((1,), (1,)), ((), ()))
    dot = functools.partial(lax.dot_general, preferred_element_type=jnp.float32)
    gate_pre = dot(gate_sel[...], gate_w[...], nn)
    up_pre = dot(up_sel[...], up_w[...], nn)
    grad_hidden = dot(down_sel[...], down_w[...], nt)
    sig = jax.nn.sigmoid(gate_pre)
    act = gate_pre * sig
    hidden = (act * up_pre).astype(jnp.bfloat16)
    gate_act = (grad_hidden * up_pre * sig * (1.0 + gate_pre * (1.0 - sig))).astype(jnp.bfloat16)
    up_act = (grad_hidden * act).astype(jnp.bfloat16)

    for slot in range(slots):
        span = slice(slot * blk, (slot + 1) * blk)
        src, sub = slot // per_dev, slot % per_dev
        g = dot(gate_sel[:, span].T, gate_act, nn) * scale_ref[0, slot, r]
        grad_refs[0][src][sub, 0] = g.astype(jnp.bfloat16)
        g = dot(up_sel[:, span].T, up_act, nn) * scale_ref[1, slot, r]
        grad_refs[1][src][sub, 0] = g.astype(jnp.bfloat16)
    hidden_t = hidden.T
    down = dot(hidden_t, down_sel[...], nn)
    for slot in range(slots):
        src, sub = slot // per_dev, slot % per_dev
        g = down[:, slot * blk : (slot + 1) * blk] * scale_ref[2, slot, r]
        grad_refs[2][src][sub, 0] = g.astype(jnp.bfloat16)

    for array, acc, left, w in ((0, in_acc, gate_act, gate_w), (1, in_acc, up_act, up_w), (2, out_acc, hidden, down_w)):
        product = dot(left, w[...], nn if array == 2 else nt)
        for slot in range(slots):
            place = rows_ref[array, slot, r]
            acc[place] += product[:, slot * blk : (slot + 1) * blk]

    @pl.when(step == pl.num_programs(0) - 1)
    def _():
        for which, acc in enumerate((out_acc, in_acc)):
            for c, ref in enumerate((own_ref, other_ref)):
                for x in range(2):
                    q = c * 2 + x

                    @pl.loop(0, nblk)
                    def _(d):
                        ref[d // per_shard, which, x, d % per_shard] = acc[d, q * tok : (q + 1) * tok, :].astype(jnp.bfloat16)


def columns(table_rows, table_scale, mine, tok_all, own_w, recv_w, base, size, prev):
    nsrc = 1 + recv_w[0].shape[0]
    _, per_dev, count, blk, _ = recv_w[0].shape
    _, shards, _, _, per_shard, tok, _ = tok_all.shape
    nblk = shards * per_shard
    slots = per_dev * nsrc
    total = 4 * tok
    whole = lambda a: pl.BlockSpec(a, lambda r, *_: (0,) * len(a), pipeline_mode=pl.Buffered(1))
    own_block = pl.BlockSpec((per_dev, 1, blk, blk), lambda r, rows, scale, at: (0, at[0] * count + base + r, 0, 0))
    recv_block = pl.BlockSpec((nsrc - 1, per_dev, 1, blk, blk), lambda r, *_: (0, 0, base + r, 0, 0))
    block = pl.BlockSpec((per_dev, 1, blk, blk), lambda r, *_: (0, r, 0, 0))
    piece = jax.ShapeDtypeStruct((per_dev, size, blk, blk), jnp.bfloat16)
    out_block = (shards, 2, 2, per_shard, tok, blk)
    bf = jnp.bfloat16
    flops = 2 * 9 * slots * size * total * blk * blk
    outs = pl.pallas_call(
        functools.partial(column_kernel, (slots, per_dev, nblk, blk, tok, base, len(prev))),
        grid_spec=pltpu.PrefetchScalarGridSpec(
            num_scalar_prefetch=3,
            grid=(size,),
            in_specs=[whole(tok_all.shape)] + [whole(out_block)] * len(prev) + [own_block] * 3 + [recv_block] * 3,
            out_specs=[block] * (3 * nsrc) + [whole(out_block)] * 2,
            scratch_shapes=[
                pltpu.VMEM((nblk, total, blk), jnp.float32),
                pltpu.VMEM((nblk, total, blk), jnp.float32),
                pltpu.VMEM((total, slots * blk), bf),
                pltpu.VMEM((total, slots * blk), bf),
                pltpu.VMEM((total, slots * blk), bf),
                pltpu.VMEM((slots * blk, blk), bf),
                pltpu.VMEM((slots * blk, blk), bf),
                pltpu.VMEM((blk, slots * blk), bf),
            ],
        ),
        out_shape=[piece] * (3 * nsrc) + [jax.ShapeDtypeStruct(out_block, bf)] * 2,
        compiler_params=pltpu.CompilerParams(vmem_limit_bytes=60 * 1024 * 1024),
        cost_estimate=pl.CostEstimate(flops=2 * flops, bytes_accessed=40 << 20, transcendentals=0),
    )(table_rows, table_scale, mine, tok_all, *prev, *own_w, *recv_w)
    grads = [outs[i * nsrc : (i + 1) * nsrc] for i in range(3)]
    return grads, outs[3 * nsrc :]


def swap(value, flip):
    return lax.ppermute(value, "fsdp", [(i, i ^ flip) for i in range(4)])


def exchanged_plan(
    tokens,
    cotangent,
    gate_values,
    gate_rows,
    gate_scale,
    up_values,
    up_rows,
    up_scale,
    down_values,
    down_cols,
    down_scale,
):
    tok, width = tokens.shape
    per_dev, local_cols, blk, _ = gate_values.shape
    count = local_cols // 4
    mine = lax.axis_index("fsdp")
    f32, bf = jnp.float32, jnp.bfloat16

    shards = lax.axis_size("tensor")
    both = jnp.stack([tokens, cotangent]).reshape(2, tok, width // blk, blk).transpose(0, 2, 1, 3)
    small = jnp.stack(
        [a.astype(f32) for a in (gate_rows, up_rows, down_cols, gate_scale, up_scale, down_scale)]
    )
    small = small.reshape(6, per_dev, 4, count).transpose(2, 0, 1, 3)
    own_w = (gate_values, up_values, down_values)
    tok_all, *recv_w, table = gather(small, both, own_w, shards)
    kept = lax.dynamic_slice_in_dim(small, mine, 1, axis=0)
    table = jnp.concatenate([kept, table]).transpose(1, 0, 2, 3).reshape(6, 4 * per_dev, count)
    table_rows = table[:3].astype(jnp.int32)
    table_scale = table[3:]
    results = [jnp.zeros((per_dev, local_cols, blk, blk), bf) for _ in own_w]
    prev, base = (), 0
    first = max(1, count * SPLIT // 10)
    chunks = []
    for size in (first, count - first):
        if size:
            grads, prev = columns(table_rows, table_scale, mine.reshape(1), tok_all, own_w, recv_w, base, size, prev)
            sent = [[p if m == 0 else swap(p, m) for m, p in enumerate(pieces)] for pieces in grads]
            chunks.append((base, sent))
            base += size
    for base, sent in chunks:
        for i, pieces in enumerate(sent):
            for m, part in enumerate(pieces):
                results[i] = lax.dynamic_update_slice_in_dim(
                    results[i], part, (mine ^ m) * count + base, axis=1
                )
    own, other = prev
    chip = (own.astype(f32) + swap(other, 1).astype(f32)).astype(bf)
    shard = lax.psum_scatter(chip, "tensor", scatter_dimension=0, tiled=False)
    done = (shard[:, 0].astype(f32) + swap(shard[:, 1], 2).astype(f32)).astype(bf)
    done = done.transpose(0, 2, 1, 3).reshape(2, tok, width)
    return (done[0], done[1], *results)


def choose_plan(mesh, *args):
    fits = mesh.shape["fsdp"] == 4 and mesh.shape["parts"] == 2 and args[2].shape[0] == 2
    fits = fits and args[2].shape[1] % 4 == 0
    plan = exchanged_plan if fits else gathered_plan
    return plan(*args)


def solution(mesh):
    plan = functools.partial(choose_plan, mesh)
    in_specs = (
        P(("parts", "fsdp"), "tensor"),
        P(("parts", "fsdp"), "tensor"),
        P("fsdp", "tensor", None, None),
        P("fsdp", "tensor"),
        P("fsdp", "tensor"),
        P("fsdp", "tensor", None, None),
        P("fsdp", "tensor"),
        P("fsdp", "tensor"),
        P("fsdp", "tensor", None, None),
        P("fsdp", "tensor"),
        P("fsdp", "tensor"),
    )
    out_specs = (
        P(("parts", "fsdp"), "tensor"),
        P(("parts", "fsdp"), "tensor"),
        P(("parts", "fsdp"), "tensor", None, None),
        P(("parts", "fsdp"), "tensor", None, None),
        P(("parts", "fsdp"), "tensor", None, None),
    )
    return jax.shard_map(plan, mesh=mesh, in_specs=in_specs, out_specs=out_specs, check_vma=False)
```

```python
import functools

import jax
import jax.numpy as jnp
from jax import lax
from jax.experimental import pallas as pl
from jax.experimental.pallas import tpu as pltpu
from jax.sharding import PartitionSpec as P


def scaled_sum(products, factors):
    return jnp.sum(products * factors.astype(jnp.float32)[None, :, :, None], axis=1)


def slot_term(selected, grads, factors):
    return (
        jnp.einsum("tkra,trb->krab", selected, grads, preferred_element_type=jnp.float32)
        * factors[:, :, None, None]
    )


def gathered_plan(
    tokens,
    cotangent,
    gate_values,
    gate_rows,
    gate_scale,
    up_values,
    up_rows,
    up_scale,
    down_values,
    down_cols,
    down_scale,
):
    block_size = gate_values.shape[-1]
    token_count = tokens.shape[0]
    tensor_count = lax.axis_size("tensor")
    nblocks = tokens.shape[1] * tensor_count // block_size
    local_blocks = nblocks // tensor_count
    gathered = lax.all_gather(tokens, "tensor", axis=1, tiled=True)
    x_blocks = gathered.reshape(token_count, nblocks, block_size)
    gate_where, up_where, down_where = (
        lax.all_gather(gate_rows, "fsdp", axis=0, tiled=True),
        lax.all_gather(up_rows, "fsdp", axis=0, tiled=True),
        lax.all_gather(down_cols, "fsdp", axis=0, tiled=True),
    )
    gate_blocks, gate_factor, up_blocks, up_factor, down_blocks, down_factor = (
        lax.all_gather(gate_values, "fsdp", axis=0, tiled=True),
        lax.all_gather(gate_scale, "fsdp", axis=0, tiled=True),
        lax.all_gather(up_values, "fsdp", axis=0, tiled=True),
        lax.all_gather(up_scale, "fsdp", axis=0, tiled=True),
        lax.all_gather(down_values, "fsdp", axis=0, tiled=True),
        lax.all_gather(down_scale, "fsdp", axis=0, tiled=True),
    )
    gate_sel = x_blocks[:, gate_where]
    up_sel = x_blocks[:, up_where]
    gate_pre = scaled_sum(
        jnp.einsum("tkra,krab->tkrb", gate_sel, gate_blocks, preferred_element_type=jnp.float32),
        gate_factor,
    )
    up_pre = scaled_sum(
        jnp.einsum("tkra,krab->tkrb", up_sel, up_blocks, preferred_element_type=jnp.float32),
        up_factor,
    )
    sigmoid_gate = jax.nn.sigmoid(gate_pre)
    activated = gate_pre * sigmoid_gate
    hidden = (activated * up_pre).astype(jnp.bfloat16)
    down_float = down_factor.astype(jnp.float32)
    down_scaled = (
        jnp.einsum("trb,krbc->krtc", hidden, down_blocks, preferred_element_type=jnp.float32)
        * down_float[:, :, None, None]
    )
    out_full = (
        jnp.zeros((nblocks, token_count, block_size), jnp.float32).at[down_where].add(down_scaled)
    )
    out_part = lax.psum_scatter(
        out_full.astype(jnp.bfloat16), "tensor", scatter_dimension=0, tiled=True
    ).astype(jnp.float32)
    layer_out = (
        jnp.transpose(out_part, (1, 0, 2))
        .reshape(token_count, local_blocks * block_size)
        .astype(jnp.bfloat16)
    )
    grad_full = lax.all_gather(cotangent, "tensor", axis=1, tiled=True).reshape(
        token_count, nblocks, block_size
    )
    down_sel = grad_full[:, down_where]
    gate_float = gate_factor.astype(jnp.float32)
    up_float = up_factor.astype(jnp.float32)
    grad_hidden = scaled_sum(
        jnp.einsum("tkrc,krbc->tkrb", down_sel, down_blocks, preferred_element_type=jnp.float32),
        down_factor,
    )
    grad_down = lax.psum_scatter(
        (
            jnp.einsum("trb,tkrc->krbc", hidden, down_sel, preferred_element_type=jnp.float32)
            * down_float[:, :, None, None]
        ).astype(jnp.bfloat16),
        "fsdp",
        scatter_dimension=0,
        tiled=True,
    )
    grad_gate_act = (
        grad_hidden * up_pre * sigmoid_gate * (1.0 + gate_pre * (1.0 - sigmoid_gate))
    ).astype(jnp.bfloat16)
    grad_up_act = (grad_hidden * activated).astype(jnp.bfloat16)
    grad_gate = lax.psum_scatter(
        slot_term(gate_sel, grad_gate_act, gate_float).astype(jnp.bfloat16),
        "fsdp",
        scatter_dimension=0,
        tiled=True,
    )
    grad_up = lax.psum_scatter(
        slot_term(up_sel, grad_up_act, up_float).astype(jnp.bfloat16),
        "fsdp",
        scatter_dimension=0,
        tiled=True,
    )
    back_gate = (
        jnp.einsum("trb,krab->krta", grad_gate_act, gate_blocks, preferred_element_type=jnp.float32)
        * gate_float[:, :, None, None]
    )
    back_up = (
        jnp.einsum("trb,krab->krta", grad_up_act, up_blocks, preferred_element_type=jnp.float32)
        * up_float[:, :, None, None]
    )
    in_full = (
        jnp.zeros((nblocks, token_count, block_size), jnp.float32)
        .at[gate_where]
        .add(back_gate)
        .at[up_where]
        .add(back_up)
    )
    in_part = lax.psum_scatter(
        in_full.astype(jnp.bfloat16), "tensor", scatter_dimension=0, tiled=True
    ).astype(jnp.float32)
    grad_tokens = (
        jnp.transpose(in_part, (1, 0, 2))
        .reshape(token_count, local_blocks * block_size)
        .astype(jnp.bfloat16)
    )
    return (layer_out, grad_tokens, grad_gate, grad_up, grad_down)


def gather_kernel(shards, small, both, wg, wu, wd, tok_all, rg, ru, rd, table, *sems):
    (z_send, z_recv, c_send, c_recv, x_send, x_recv, w_send, w_recv, y_send, y_recv, n_send, n_recv, s_send, s_recv, here) = sems
    part, t, f = lax.axis_index("parts"), lax.axis_index("tensor"), lax.axis_index("fsdp")
    flip = [f, (f // 2) * 2 + 1 - f % 2, (f + 2) % 4, ((f + 2) % 4 // 2) * 2 + 1 - f % 2]
    count = rg.shape[2]
    last = shards - 1
    weights = ((wg, rg), (wu, ru), (wd, rd))

    def to(where, src, dst, send, recv):
        return pltpu.make_async_remote_copy(
            src_ref=src, dst_ref=dst, send_sem=send, recv_sem=recv,
            device_id=where, device_id_type=pl.DeviceIdType.MESH,
        )

    def across(m):
        return (part, t, flip[m])

    over = (1 - part, t, f)
    ups = ((part, t + 1, f), (part, t - 1, f))
    more = (t < last, t > 0)

    barrier = pltpu.get_barrier_semaphore()
    for m in (1, 2, 3):
        pl.semaphore_signal(barrier, inc=1, device_id=across(m), device_id_type=pl.DeviceIdType.MESH)
    pl.semaphore_signal(barrier, inc=1, device_id=over, device_id_type=pl.DeviceIdType.MESH)
    for way in range(2):
        @pl.when(more[way])
        def _():
            pl.semaphore_signal(barrier, inc=1, device_id=ups[way], device_id_type=pl.DeviceIdType.MESH)
    ends = jnp.logical_or(t == 0, t == last)

    @pl.when(ends)
    def _():
        pl.semaphore_wait(barrier, 5)

    @pl.when(jnp.logical_not(ends))
    def _():
        pl.semaphore_wait(barrier, 6)

    def z_copy(way, src, x, own=False):
        source = both if own else tok_all.at[0, src, x]
        return to(ups[way], source, tok_all.at[0, src, x], z_send.at[way, src, x], z_recv.at[way, src, x])

    def c_copy(src, x, own=False):
        source = both if own else tok_all.at[0, src, x]
        return to(across(1), source, tok_all.at[1, src, x], c_send.at[src, x], c_recv.at[src, x])

    x_copy = to(across(2), both, tok_all.at[0, t, 1], x_send, x_recv)
    keep = pltpu.make_async_copy(both, tok_all.at[0, t, 0], here)
    x_copy.start()
    for way in range(2):
        @pl.when(more[way])
        def _():
            z_copy(way, t, 0, True).start()
    tables = [
        to(across(m), small.at[flip[m]], table.at[m - 1], s_send.at[m - 1], s_recv.at[m - 1])
        for m in (1, 2, 3)
    ]
    for c in tables:
        c.start()
    c_copy(t, 0, True).start()
    w_copies, y_copies, y_waits, n_copies = [], [], [], []
    for w, r in weights:
        for m in (2, 3):
            j = len(w_copies)
            w_copies.append(to(across(m), w.at[part, pl.ds(flip[m] * count, count)], r.at[m - 1, part], w_send.at[j], w_recv.at[j]))
            y_copies.append(to(over, r.at[m - 1, part], r.at[m - 1, part], y_send.at[j], y_recv.at[j]))
            y_waits.append(to(over, r.at[m - 1, part], r.at[m - 1, 1 - part], y_send.at[j], y_recv.at[j]))
        for k in range(2):
            j = len(n_copies)
            n_copies.append(to(across(1), w.at[k, pl.ds(flip[1] * count, count)], r.at[0, k], n_send.at[j], n_recv.at[j]))
    for c in w_copies:
        c.start()
    for c in n_copies:
        c.start()
    keep.start()

    x_copy.wait_recv()
    for way in range(2):
        @pl.when(more[way])
        def _():
            z_copy(way, t, 1).start()
    c_copy(t, 1).start()

    def arrive(step, x):
        for way in range(2):
            src = t - step if way == 0 else t + step

            @pl.when(src >= 0 if way == 0 else src <= last)
            def _():
                z_copy(way, src, x).wait_recv()

                @pl.when(more[way])
                def _():
                    z_copy(way, src, x).start()

                c_copy(src, x).start()

    def relay(j):
        w_copies[j].wait_recv()
        y_copies[j].start()

    order = [(s, x) for s in range(1, shards) for x in range(2)]
    done = 0
    for i, (s, x) in enumerate(order):
        arrive(s, x)
        while done < len(w_copies) and done < 2 * i + 1:
            relay(done)
            done += 1
    while done < len(w_copies):
        relay(done)
        done += 1

    for way in range(2):
        for s in range(shards):
            src = t - s if way == 0 else t + s

            @pl.when(jnp.logical_and(src >= 0 if way == 0 else src <= last, more[way]))
            def _():
                for x in range(2):
                    z_copy(way, src, x, s == 0 and x == 0).wait_send()
    for src in range(shards):
        for x in range(2):
            c_copy(src, x).wait_send()
            c_copy(src, x).wait_recv()
    for c in tables + n_copies:
        c.wait_send()
        c.wait_recv()
    x_copy.wait_send()
    for c in w_copies + y_copies:
        c.wait_send()
    for c in y_waits:
        c.wait_recv()
    keep.wait()


def gather(small, both, weights, shards):
    per_dev, local_cols, blk, _ = weights[0].shape
    count = local_cols // 4
    bf = jnp.bfloat16
    dma = lambda *a: pltpu.SemaphoreType.DMA(a)
    received = jax.ShapeDtypeStruct((3, per_dev, count, blk, blk), bf)
    anywhere = pl.BlockSpec(memory_space=pl.ANY)
    z = (2, shards, 2)
    c = (shards, 2)
    one = pltpu.SemaphoreType.DMA
    return pl.pallas_call(
        functools.partial(gather_kernel, shards),
        out_shape=[
            jax.ShapeDtypeStruct((2, shards, 2) + both.shape, bf),
            received, received, received,
            jax.ShapeDtypeStruct((3,) + small.shape[1:], jnp.float32),
        ],
        in_specs=[anywhere] * 5,
        out_specs=[anywhere] * 5,
        scratch_shapes=[dma(*z), dma(*z), dma(*c), dma(*c), one, one, dma(6), dma(6), dma(6), dma(6), dma(6), dma(6), dma(3), dma(3), one],
        compiler_params=pltpu.CompilerParams(collective_id=0, has_side_effects=True),
    )(small, both, *weights)


def column_kernel(shape, backward, rows_ref, scale_ref, mine_ref, tok_ref, *refs):
    slots, per_dev, nblk, blk, tok = shape
    nsrc = slots // per_dev
    own_w, recv_w, refs = refs[:3], refs[3:6], refs[6:]
    if backward:
        gate_pre_ref, up_pre_ref = refs[:2]
        grad_refs = [refs[2 : 2 + nsrc], refs[2 + nsrc : 2 + 2 * nsrc], ()]
        own_ref, other_ref = refs[2 + 2 * nsrc : 4 + 2 * nsrc]
        scratch = refs[4 + 2 * nsrc :]
    else:
        grad_refs = [(), (), refs[:nsrc]]
        gate_pre_ref, up_pre_ref, own_ref, other_ref = refs[nsrc : nsrc + 4]
        scratch = refs[nsrc + 4 :]
    acc, gate_sel, up_sel, down_sel, gate_w, up_w, down_w = scratch
    r = pl.program_id(0)
    per_shard = tok_ref.shape[4]

    @pl.when(r == 0)
    def _():
        acc[...] = jnp.zeros_like(acc)

    def load(which, slot, array, sel):
        place = rows_ref[array, slot, r]
        shard, block = place // per_shard, place % per_shard
        lanes = slice(slot * blk, (slot + 1) * blk)
        for c in range(2):
            for x in range(2):
                q = c * 2 + x
                sel[q * tok : (q + 1) * tok, lanes] = tok_ref[c, shard, x, which, block]

    def scaled(array, slot):
        src, sub = slot // per_dev, slot % per_dev
        value = recv_w[array][src - 1, sub, 0] if src else own_w[array][sub, 0]
        return (value.astype(jnp.float32) * scale_ref[array, slot, r]).astype(jnp.bfloat16)

    for slot in range(slots):
        span = slice(slot * blk, (slot + 1) * blk)
        load(0, slot, 0, gate_sel)
        load(0, slot, 1, up_sel)
        load(1, slot, 2, down_sel)
        gate_w[span, :] = scaled(0, slot)
        up_w[span, :] = scaled(1, slot)
        down_w[:, span] = scaled(2, slot)

    nn = (((1,), (0,)), ((), ()))
    nt = (((1,), (1,)), ((), ()))
    dot = functools.partial(lax.dot_general, preferred_element_type=jnp.float32)

    def add(array, left, w, form):
        product = dot(left, w[...], form)
        for slot in range(slots):
            acc[rows_ref[array, slot, r]] += product[:, slot * blk : (slot + 1) * blk]

    if backward:
        gate_pre, up_pre = gate_pre_ref[0], up_pre_ref[0]
        grad_hidden = dot(down_sel[...], down_w[...], nt)
        sig = jax.nn.sigmoid(gate_pre)
        act = gate_pre * sig
        gate_act = (grad_hidden * up_pre * sig * (1.0 + gate_pre * (1.0 - sig))).astype(jnp.bfloat16)
        up_act = (grad_hidden * act).astype(jnp.bfloat16)
        for slot in range(slots):
            span = slice(slot * blk, (slot + 1) * blk)
            src, sub = slot // per_dev, slot % per_dev
            g = dot(gate_sel[:, span].T, gate_act, nn) * scale_ref[0, slot, r]
            grad_refs[0][src][sub, 0] = g.astype(jnp.bfloat16)
            g = dot(up_sel[:, span].T, up_act, nn) * scale_ref[1, slot, r]
            grad_refs[1][src][sub, 0] = g.astype(jnp.bfloat16)
        add(0, gate_act, gate_w, nt)
        add(1, up_act, up_w, nt)
    else:
        gate_pre = dot(gate_sel[...], gate_w[...], nn)
        up_pre = dot(up_sel[...], up_w[...], nn)
        gate_pre_ref[0], up_pre_ref[0] = gate_pre, up_pre
        hidden = (gate_pre * jax.nn.sigmoid(gate_pre) * up_pre).astype(jnp.bfloat16)
        down = dot(hidden.T, down_sel[...], nn)
        for slot in range(slots):
            src, sub = slot // per_dev, slot % per_dev
            g = down[:, slot * blk : (slot + 1) * blk] * scale_ref[2, slot, r]
            grad_refs[2][src][sub, 0] = g.astype(jnp.bfloat16)
        add(2, hidden, down_w, nn)

    @pl.when(r == pl.num_programs(0) - 1)
    def _():
        for c, ref in enumerate((own_ref, other_ref)):
            for x in range(2):
                q = c * 2 + x

                @pl.loop(0, nblk)
                def _(d):
                    ref[d // per_shard, x, d % per_shard] = acc[d, q * tok : (q + 1) * tok, :].astype(jnp.bfloat16)


def columns(table_rows, table_scale, mine, tok_all, own_w, recv_w, kept):
    nsrc = 1 + recv_w[0].shape[0]
    _, per_dev, count, blk, _ = recv_w[0].shape
    _, shards, _, _, per_shard, tok, _ = tok_all.shape
    nblk = shards * per_shard
    slots = per_dev * nsrc
    total = 4 * tok
    bf, f32 = jnp.bfloat16, jnp.float32
    whole = lambda a: pl.BlockSpec(a, lambda r, *_: (0,) * len(a), pipeline_mode=pl.Buffered(1))
    own_block = pl.BlockSpec((per_dev, 1, blk, blk), lambda r, rows, scale, at: (0, at[0] * count + r, 0, 0))
    recv_block = pl.BlockSpec((nsrc - 1, per_dev, 1, blk, blk), lambda r, *_: (0, 0, r, 0, 0))
    block = pl.BlockSpec((per_dev, 1, blk, blk), lambda r, *_: (0, r, 0, 0))
    piece = jax.ShapeDtypeStruct((per_dev, count, blk, blk), bf)
    pre_block = [pl.BlockSpec((1, total, blk), lambda r, *_: (r, 0, 0))] * 2
    pre = [jax.ShapeDtypeStruct((count, total, blk), f32)] * 2
    out_block = (shards, 2, per_shard, tok, blk)
    sums = [jax.ShapeDtypeStruct(out_block, bf)] * 2
    backward = len(kept) > 0
    flops = 2 * 9 * slots * count * total * blk * blk
    return pl.pallas_call(
        functools.partial(column_kernel, (slots, per_dev, nblk, blk, tok), backward),
        grid_spec=pltpu.PrefetchScalarGridSpec(
            num_scalar_prefetch=3,
            grid=(count,),
            in_specs=[whole(tok_all.shape)] + [own_block] * 3 + [recv_block] * 3 + (pre_block if backward else []),
            out_specs=([block] * (2 * nsrc) if backward else [block] * nsrc + pre_block) + [whole(out_block)] * 2,
            scratch_shapes=[
                pltpu.VMEM((nblk, total, blk), f32),
                pltpu.VMEM((total, slots * blk), bf),
                pltpu.VMEM((total, slots * blk), bf),
                pltpu.VMEM((total, slots * blk), bf),
                pltpu.VMEM((slots * blk, blk), bf),
                pltpu.VMEM((slots * blk, blk), bf),
                pltpu.VMEM((blk, slots * blk), bf),
            ],
        ),
        out_shape=([piece] * (2 * nsrc) if backward else [piece] * nsrc + pre) + sums,
        compiler_params=pltpu.CompilerParams(vmem_limit_bytes=60 * 1024 * 1024),
        cost_estimate=pl.CostEstimate(flops=flops, bytes_accessed=40 << 20, transcendentals=0),
    )(table_rows, table_scale, mine, tok_all, *own_w, *recv_w, *kept)


def swap(value, flip):
    return lax.ppermute(value, "fsdp", [(i, i ^ flip) for i in range(4)])


def exchanged_plan(
    tokens,
    cotangent,
    gate_values,
    gate_rows,
    gate_scale,
    up_values,
    up_rows,
    up_scale,
    down_values,
    down_cols,
    down_scale,
):
    tok, width = tokens.shape
    per_dev, local_cols, blk, _ = gate_values.shape
    count = local_cols // 4
    mine = lax.axis_index("fsdp")
    f32, bf = jnp.float32, jnp.bfloat16

    shards = lax.axis_size("tensor")
    both = jnp.stack([tokens, cotangent]).reshape(2, tok, width // blk, blk).transpose(0, 2, 1, 3)
    small = jnp.stack(
        [a.astype(f32) for a in (gate_rows, up_rows, down_cols, gate_scale, up_scale, down_scale)]
    )
    small = small.reshape(6, per_dev, 4, count).transpose(2, 0, 1, 3)
    own_w = (gate_values, up_values, down_values)
    tok_all, *recv_w, table = gather(small, both, own_w, shards)
    kept = lax.dynamic_slice_in_dim(small, mine, 1, axis=0)
    table = jnp.concatenate([kept, table]).transpose(1, 0, 2, 3).reshape(6, 4 * per_dev, count)
    table_rows = table[:3].astype(jnp.int32)
    table_scale = table[3:]

    def home(pieces):
        result = jnp.zeros((per_dev, local_cols, blk, blk), bf)
        for m, part in enumerate(pieces):
            result = lax.dynamic_update_slice_in_dim(result, part, (mine ^ m) * count, axis=1)
        return result

    def send(pieces):
        return [p if m == 0 else swap(p, m) for m, p in enumerate(pieces)]

    def chip_sum(own, other):
        return (own.astype(f32) + swap(other, 1).astype(f32)).astype(bf)

    def scatter(chip):
        return lax.psum_scatter(chip, "tensor", scatter_dimension=0, tiled=False)

    def finish(shard):
        total = (shard[0].astype(f32) + swap(shard[1], 2).astype(f32)).astype(bf)
        return total.transpose(1, 0, 2).reshape(tok, width)

    place = mine.reshape(1)
    *down_pieces, gate_pre, up_pre, own, other = columns(table_rows, table_scale, place, tok_all, own_w, recv_w, ())
    chip = chip_sum(own, other)
    down_sent = send(down_pieces)
    chip, table_scale = lax.optimization_barrier((chip, table_scale))
    out_shard = scatter(chip)
    late = columns(table_rows, table_scale, place, tok_all, own_w, recv_w, (gate_pre, up_pre))
    gate_sent, up_sent = send(late[:4]), send(late[4:8])
    in_shard = scatter(chip_sum(late[8], late[9]))
    return (finish(out_shard), finish(in_shard), home(gate_sent), home(up_sent), home(down_sent))


def choose_plan(mesh, *args):
    fits = mesh.shape["fsdp"] == 4 and mesh.shape["parts"] == 2 and args[2].shape[0] == 2
    fits = fits and args[2].shape[1] % 4 == 0
    plan = exchanged_plan if fits else gathered_plan
    return plan(*args)


def solution(mesh):
    plan = functools.partial(choose_plan, mesh)
    in_specs = (
        P(("parts", "fsdp"), "tensor"),
        P(("parts", "fsdp"), "tensor"),
        P("fsdp", "tensor", None, None),
        P("fsdp", "tensor"),
        P("fsdp", "tensor"),
        P("fsdp", "tensor", None, None),
        P("fsdp", "tensor"),
        P("fsdp", "tensor"),
        P("fsdp", "tensor", None, None),
        P("fsdp", "tensor"),
        P("fsdp", "tensor"),
    )
    out_specs = (
        P(("parts", "fsdp"), "tensor"),
        P(("parts", "fsdp"), "tensor"),
        P(("parts", "fsdp"), "tensor", None, None),
        P(("parts", "fsdp"), "tensor", None, None),
        P(("parts", "fsdp"), "tensor", None, None),
    )
    return jax.shard_map(plan, mesh=mesh, in_specs=in_specs, out_specs=out_specs, check_vma=False)
```
